128 devices in a mesh: subset: 8 (over y, z_lo), tile: 16 (over z_hi, x, core).
Axes of the slice: x: 4, y: 4, z: 4 (z_hi: 2, z_lo: 2; z = z_hi * 2 + z_lo), core: 2. Of those that a mesh axis runs over, the one named last changes fastest.
Arguments:
- start_volume: bfloat16 [8, 64, 65536], P(None, None, 'tile'), may hold values from 0 to 2
- measured: bfloat16 [8, 8, 64, 2048], P('subset'), may hold values from 6528 to 26112
- system_values: bfloat16 [8, 2048, 65536], P('subset', None, 'tile'), may hold values from 0.05 to 2088.96, as said below
- block_pattern: int32 [8, 16, 512], P('subset', None, 'tile'), may hold values from 0 to 1, as said below
- subset_order: int32 [64, 8], replicated, may hold values from 0 to 7, each once within a row
Outputs:
- volume_out: bfloat16 [8, 64, 65536], P(None, None, 'tile')
The draws below stay inside these ranges and needn't reach their ends.
Inputs may be any that keep to these rules, and one draw needn't show every extreme that they name: `block_pattern`: each entry is 0 or 1; every block row and every block column of each subset's matrix within every 4096-voxel tile holds at least one 1. `system_values`: positive entries. `subset_order`: each row is a permutation of the 8 subsets.
All inputs are finite; a program needn't handle non-finite values.
Results may differ from the reference program's by a relative error of at most 0.0034.
Values may be sent and summed in bfloat16 or wider, within the bound.
A program may use at most 128 MiB of HBM per device.

```python
import jax
import jax.numpy as jnp
from jax import lax

TILE_VOX = 4096
SUBSET_RAY_COUNT = 2048
BLOCK_SIDE = 128
SLICES = 64
SWEEP_PASSES = 4
ANGLE_SUBSETS = 8
FRONTS = 8
SLICE_VOX = 65536


def draw_system_values(key, part):
    angle_count = 8
    bins_count = SUBSET_RAY_COUNT // angle_count
    floor_key = jax.random.fold_in(key, 21)
    path_key = jax.random.fold_in(key, 22)
    bin_key = jax.random.fold_in(key, 23)
    floor_part = jax.random.uniform(floor_key, (ANGLE_SUBSETS, angle_count, bins_count, SLICE_VOX), jnp.float32, 0.05, 0.25)
    path_part = jax.random.uniform(path_key, (ANGLE_SUBSETS, angle_count, bins_count, SLICE_VOX), jnp.float32, 0.3, 0.9) * bins_count
    voxel_bins = jax.random.randint(bin_key, (ANGLE_SUBSETS, angle_count, 1, SLICE_VOX), 0, bins_count)
    detector = jnp.arange(bins_count, dtype=jnp.int32)[None, None, :, None]
    values = jnp.where(voxel_bins == detector, path_part, floor_part)
    values = values.reshape(ANGLE_SUBSETS, SUBSET_RAY_COUNT, SLICE_VOX)
    columns = jnp.arange(SLICE_VOX, dtype=jnp.float32) / SLICE_VOX
    ramp = 3.0 ** columns
    return (values * ramp[None, None, :]).astype(jnp.bfloat16)


def draw_block_pattern(key, part):
    blocks_per_row = SUBSET_RAY_COUNT // BLOCK_SIDE
    col_blocks = SLICE_VOX // BLOCK_SIDE
    coins = jax.random.randint(jax.random.fold_in(key, 11), (ANGLE_SUBSETS, blocks_per_row, col_blocks), 0, 100)
    base = (coins < 37).astype(jnp.int32)
    local_cols = jnp.arange(col_blocks, dtype=jnp.int32) % (TILE_VOX // BLOCK_SIDE)
    forced_rows = local_cols % blocks_per_row
    forced = (jnp.arange(blocks_per_row, dtype=jnp.int32)[:, None] == forced_rows[None, :]).astype(jnp.int32)
    return jnp.maximum(base, forced[None, :, :])


def shard_levels(key, shape, cuts, smallest, top_value):
    gain, own = 1.0, jax.random.fold_in(key, 6)
    for dim, blocks in cuts:
        steps = jnp.exp(jax.random.uniform(jax.random.fold_in(own, dim), (blocks,), jnp.float32, smallest / len(cuts), top_value / len(cuts)))
        gain = gain * jnp.repeat(steps, shape[dim] // blocks).reshape([-1 if axis == dim else 1 for axis in range(len(shape))])
    return gain


def setup_inputs(seed: int = 0) -> dict:
    splits = jax.random.split(jax.random.key(seed), 6)
    start_volume = jnp.clip(2.0 * jax.random.uniform(splits[0], (FRONTS, SLICES, SLICE_VOX), jnp.float32) ** shard_levels(splits[0], (FRONTS, SLICES, SLICE_VOX), ((2, 16),), -0.2, 0.2), 0.0, 2.0).astype(jnp.bfloat16)
    measured = jnp.clip(6528.0 + 19584.0 * jax.random.uniform(splits[1], (ANGLE_SUBSETS, FRONTS, SLICES, SUBSET_RAY_COUNT), jnp.float32) ** shard_levels(splits[1], (ANGLE_SUBSETS, FRONTS, SLICES, SUBSET_RAY_COUNT), ((0, 8),), -0.2, 0.2), 6528.0, 26112.0).astype(jnp.bfloat16)
    system_values = draw_system_values(jax.random.fold_in(splits[5], 71), 0)
    block_pattern = draw_block_pattern(jax.random.fold_in(splits[5], 71), 0)
    subset_order = jax.vmap(lambda own: jax.random.permutation(own, ANGLE_SUBSETS))(jax.random.split(splits[4], SLICES)).reshape((SLICES, ANGLE_SUBSETS)).astype(jnp.int32)
    return {"start_volume": start_volume, "measured": measured, "system_values": system_values, "block_pattern": block_pattern, "subset_order": subset_order}


def expand(pattern):
    return jnp.repeat(jnp.repeat(pattern, BLOCK_SIDE, 0), BLOCK_SIDE, 1)


def reference(start_volume, measured, system_values, block_pattern, subset_order):
    volume_all = start_volume.astype(jnp.float32)
    slice_index = jnp.arange(SLICES, dtype=jnp.int32)
    front_index = jnp.arange(FRONTS, dtype=jnp.int32)
    for slice_portion in range(SWEEP_PASSES):
        updated_all = volume_all
        for subset_now in range(ANGLE_SUBSETS):
            hits = ((subset_order + slice_portion) % ANGLE_SUBSETS == subset_now).astype(jnp.int32)
            chosen = jnp.sum(hits * front_index[None, :], axis=1).astype(jnp.int32)
            matrix = system_values[subset_now] * expand(block_pattern[subset_now]).astype(system_values.dtype)
            row_sums = jnp.sum(matrix, axis=1, dtype=jnp.float32)
            column_sums = jnp.sum(matrix, axis=0, dtype=jnp.float32)
            volume = volume_all[chosen, slice_index]
            projected = lax.dot_general(volume.astype(matrix.dtype), matrix, (((1,), (1,)), ((), ())), preferred_element_type=jnp.float32)
            destination_rows = measured[subset_now][chosen, slice_index].astype(jnp.float32)
            residue = ((destination_rows - projected) / row_sums[None, :]).astype(matrix.dtype)
            spread_back = jnp.dot(residue, matrix, preferred_element_type=jnp.float32)
            updated_all = updated_all.at[chosen, slice_index].set(volume + spread_back / column_sums[None, :])
        volume_all = updated_all
    return volume_all.astype(start_volume.dtype)
```

```python
import functools

import jax
import jax.numpy as jnp
from jax import lax
from jax.experimental import pallas as pl
from jax.experimental.pallas import tpu as pltpu
from jax.sharding import PartitionSpec as P

MESH = pl.DeviceIdType.MESH
F32 = jnp.float32
BF16 = jnp.bfloat16
SIDE = 128
PASSES = 4
ONES = 16
NT = (((1,), (1,)), ((), ()))
NN = (((1,), (0,)), ((), ()))


def dot(a, b, dims):
    return lax.dot_general(a, b, dims, preferred_element_type=F32)


def sweep_kernel(
    tiles, order_ref, mask_ref, start_hbm, meas_hbm, sys_hbm, out_hbm,
    a_ref, start_ref, vb_ref, meas_ref, dest_ref, rows_ref, inv_ref, part, recv, resid,
    hi_out, lo_out, hi_in, lo_in, acc, gat,
    a_sem, io_sem, rs_send, rs_recv, ag_send, ag_recv, hop_send, hop_recv, fin_send, fin_recv, out_sem,
):
    me_s, me_t = lax.axis_index("subset"), lax.axis_index("tile")
    subsets = order_ref.shape[1]
    slices = order_ref.shape[0]
    rays, vox = a_ref.shape
    chunk = rays // tiles
    pair = 2 * chunk
    pairs = rays // pair
    chunks = hop_send.shape[2]
    width = vox // chunks

    def tile_at(d):
        return lax.rem(me_t + d, tiles)

    def subset_at(d):
        return lax.rem(me_s + d, subsets)

    def remote(src, dst, send, recv_, s, t):
        return pltpu.make_async_remote_copy(
            src_ref=src, dst_ref=dst, send_sem=send, recv_sem=recv_,
            device_id=(s, t), device_id_type=MESH,
        )

    def cols(n):
        return pl.ds(pl.multiple_of(n * width, width), width)

    def rays_of(c):
        return pl.ds(pl.multiple_of(c * chunk, chunk), chunk)

    start_copy = pltpu.make_async_copy(start_hbm, start_ref, io_sem.at[0])
    start_copy.start()
    half = lax.div(me_t, 2)

    def block_rows(i):
        return pl.ds(pl.multiple_of(lax.rem(half + i, pairs) * pair, pair), pair)

    def matrix_copy(i):
        return pltpu.make_async_copy(
            sys_hbm.at[0, block_rows(i), :], a_ref.at[block_rows(i), :], a_sem.at[i]
        )

    for i in range(pairs):
        matrix_copy(i).start()
    meas_copy = pltpu.make_async_copy(
        meas_hbm.at[0, :, :, rays_of(me_t)], meas_ref, io_sem.at[1]
    )
    meas_copy.start()

    barrier = pltpu.get_barrier_semaphore()
    for d in range(1, tiles):
        pl.semaphore_signal(barrier, inc=1, device_id=(me_s, tile_at(d)), device_id_type=MESH)
    for d in range(1, subsets):
        pl.semaphore_signal(barrier, inc=1, device_id=(subset_at(d), me_t), device_id_type=MESH)

    vb_ref[slices:, :] = jnp.ones((ONES, vox), BF16)
    resid[0, slices:, :] = jnp.ones((ONES, rays), BF16)

    start_copy.wait()

    @pl.loop(0, chunks)
    def _(n):
        total = jnp.zeros((slices, width), F32)
        for f in range(subsets):
            weight = (order_ref[:, f : f + 1] == me_s).astype(F32)
            total += weight * start_ref[f, :, cols(n)].astype(F32)
        vb_ref[:slices, cols(n)] = total.astype(BF16)

    pl.semaphore_wait(barrier, tiles - 1 + subsets - 1)

    def rs_copy(j, d, c, height):
        return remote(
            part.at[c, pl.ds(0, height), :], recv.at[j, d, pl.ds(0, height), :],
            rs_send.at[d], rs_recv.at[j, d], me_s, tile_at(d),
        )

    @pl.loop(0, pairs)
    def _(i):
        matrix_copy(i).wait()
        b = lax.rem(half + i, pairs)
        per_pair = pair // SIDE
        for q in range(per_pair):
            mask = jnp.broadcast_to(mask_ref[pl.ds(b * per_pair + q, 1), :], (16, vox)).astype(BF16)
            for u in range(SIDE // 16):
                here = pl.ds(pl.multiple_of(b * pair + q * SIDE + u * 16, 16), 16)
                a_ref[here, :] = a_ref[here, :] * mask
        p = dot(vb_ref[...], a_ref[block_rows(i), :], NT)
        sums = p[slices:, :]
        high = sums.astype(BF16)
        rest = sums - high.astype(F32)
        mid = rest.astype(BF16)
        low = (rest - mid.astype(F32)).astype(BF16)
        row = lax.broadcasted_iota(jnp.int32, sums.shape, 0)
        packed = jnp.where(
            row == 0, high.astype(F32),
            jnp.where(row == 1, mid.astype(F32), jnp.where(row == 2, low.astype(F32), 0.0)),
        ).astype(BF16)
        for h in range(2):
            c = 2 * b + h
            part[c, pl.ds(0, slices), :] = p[:slices, h * chunk : (h + 1) * chunk].astype(BF16)
            part[c, pl.ds(slices, ONES), :] = packed[:, h * chunk : (h + 1) * chunk]
            d = lax.rem(c + tiles - me_t, tiles)

            @pl.when(d != 0)
            def _():
                rs_copy(0, d, c, slices + ONES).start()

    meas_copy.wait()
    for j in range(PASSES):
        source = lax.rem(me_s + subsets - j, subsets)
        total = jnp.zeros((slices, chunk), F32)
        for f in range(subsets):
            weight = (order_ref[:, f : f + 1] == source).astype(F32)
            total += weight * meas_ref[f].astype(F32)
        dest_ref[j] = total

    def ag_copy(j, d):
        here = resid.at[j, pl.ds(0, slices), rays_of(me_t)]
        return remote(here, here, ag_send.at[d], ag_recv.at[j, d], me_s, tile_at(d))

    def ag_arrival(j, d):
        here = resid.at[j, pl.ds(0, slices), rays_of(lax.rem(me_t + tiles - d, tiles))]
        return remote(here, here, ag_send.at[d], ag_recv.at[j, d], me_s, tile_at(d))

    def hi_copy(j, n):
        return remote(
            hi_out.at[j, :, cols(n)], hi_in.at[j, :, cols(n)],
            hop_send.at[j, 0, n], hop_recv.at[j, 0, n], subset_at(1), me_t,
        )

    def lo_copy(j, n):
        return remote(
            lo_out.at[j, :, cols(n)], lo_in.at[j, :, cols(n)],
            hop_send.at[j, 1, n], hop_recv.at[j, 1, n], subset_at(1), me_t,
        )

    zp = me_s + 1 - 2 * lax.rem(me_s, 2)
    yp, ym, y2 = subset_at(2), subset_at(subsets - 2), subset_at(subsets // 2)
    zp_p = lax.rem(zp + 2, subsets)
    zp_m = lax.rem(zp + subsets - 2, subsets)
    zp_2 = lax.rem(zp + subsets // 2, subsets)

    def fin_copy(kind, block, n, target):
        here = gat.at[block, :, cols(n)]
        return remote(here, here, fin_send.at[kind, n], fin_recv.at[kind, n], target, me_t)

    for j in range(PASSES):
        height = slices + ONES if j == 0 else slices
        if j > 0:
            acc[...] = jnp.zeros_like(acc)

            @pl.loop(0, chunks)
            def _(n):
                hi_copy(j - 1, n).wait_recv()
                acc[...] += dot(hi_in[j - 1, :, cols(n)], a_ref[:, cols(n)], NT)

            for c in range(tiles):
                part[c, pl.ds(0, slices), :] = acc[:, c * chunk : (c + 1) * chunk].astype(BF16)
            for d in range(1, tiles):
                rs_copy(j, d, tile_at(d), slices).start()

            @pl.loop(0, chunks // 2)
            def _(n):
                lo_copy(j - 1, n).start()

        total = part[me_t].astype(F32) if j == 0 else part[me_t, pl.ds(0, slices), :].astype(F32)
        for d in range(1, tiles):
            rs_copy(j, d, tile_at(d), height).wait_recv()
            total += recv[j, d, pl.ds(0, height), :].astype(F32)
        if j == 0:
            rows_ref[...] = jnp.sum(total[slices:, :], axis=0, keepdims=True)
        value = (dest_ref[j] - total[:slices, :]) / rows_ref[...]
        resid[j, pl.ds(0, slices), rays_of(me_t)] = value.astype(BF16)
        for d in range(1, tiles):
            ag_copy(j, d).start()
        if j > 0:
            @pl.loop(chunks // 2, chunks)
            def _(n):
                lo_copy(j - 1, n).start()
        for d in range(1, tiles):
            rs_copy(j, d, tile_at(d), height).wait_send()
        for d in range(1, tiles):
            ag_arrival(j, d).wait_recv()

        @pl.loop(0, chunks)
        def _(n):
            here = cols(n)
            if j == 0:
                back = dot(resid[0], a_ref[:, here], NN)
                inv = 1.0 / back[slices : slices + 1, :]
                inv_ref[:, here] = inv
                base = vb_ref[:slices, here].astype(F32)
            else:
                back = dot(resid[j, pl.ds(0, slices), :], a_ref[:, here], NN)
                inv = inv_ref[:, here]
                lo_copy(j - 1, n).wait_recv()
                base = hi_in[j - 1, :, here].astype(F32) + lo_in[j - 1, :, here].astype(F32)
            volume = base + back[:slices, :] * inv
            high = volume.astype(BF16)
            if j + 1 < PASSES:
                hi_out[j, :, here] = high
                lo_out[j, :, here] = (volume - high.astype(F32)).astype(BF16)
                hi_copy(j, n).start()
            else:
                gat[me_s, :, here] = high
                fin_copy(0, me_s, n, zp).start()
                fin_copy(1, me_s, n, yp).start()
                fin_copy(2, me_s, n, ym).start()

        for d in range(1, tiles):
            ag_copy(j, d).wait_send()

    @pl.loop(0, chunks)
    def _(n):
        fin_copy(1, ym, n, me_s).wait_recv()
        fin_copy(2, yp, n, me_s).wait_recv()

        @pl.when(lax.rem(n, 2) == 0)
        def _():
            fin_copy(3, ym, n, yp).start()

        @pl.when(lax.rem(n, 2) == 1)
        def _():
            fin_copy(3, yp, n, ym).start()

    @pl.loop(0, chunks)
    def _(n):
        fin_copy(0, zp, n, me_s).wait_recv()
        fin_copy(4, zp, n, yp).start()
        fin_copy(5, zp, n, ym).start()

    def out_copy(block, i):
        return pltpu.make_async_copy(gat.at[block], out_hbm.at[block], out_sem.at[i])

    for i, block in enumerate((me_s, zp, yp, ym)):
        out_copy(block, i).start()

    @pl.loop(0, chunks)
    def _(n):
        fin_copy(3, y2, n, me_s).wait_recv()
        fin_copy(6, y2, n, zp).start()

    out_copy(y2, 4).start()

    @pl.loop(0, chunks)
    def _(n):
        fin_copy(4, zp_m, n, me_s).wait_recv()
        fin_copy(5, zp_p, n, me_s).wait_recv()

    out_copy(zp_m, 5).start()
    out_copy(zp_p, 6).start()

    @pl.loop(0, chunks)
    def _(n):
        fin_copy(6, zp_2, n, me_s).wait_recv()

    out_copy(zp_2, 7).start()

    @pl.loop(0, chunks)
    def _(n):
        for kind in range(7):
            fin_copy(kind, me_s, n, zp).wait_send()
        for j in range(PASSES - 1):
            hi_copy(j, n).wait_send()
            lo_copy(j, n).wait_send()

    for i, block in enumerate((me_s, zp, yp, ym, y2, zp_m, zp_p, zp_2)):
        out_copy(block, i).wait()


def sweep(tiles, chunks, order, mask, start, meas, system):
    subsets, slices, vox = start.shape
    rays = system.shape[1]
    chunk = rays // tiles
    hops = PASSES - 1
    dma = pltpu.SemaphoreType.DMA
    vmem = pl.BlockSpec(memory_space=pltpu.VMEM)
    hbm = pl.BlockSpec(memory_space=pl.ANY)
    return pl.pallas_call(
        functools.partial(sweep_kernel, tiles),
        out_shape=jax.ShapeDtypeStruct((subsets, slices, vox), BF16),
        in_specs=[vmem, vmem, hbm, hbm, hbm],
        out_specs=hbm,
        scratch_shapes=[
            pltpu.VMEM((rays, vox), BF16),
            pltpu.VMEM((subsets, slices, vox), BF16),
            pltpu.VMEM((slices + ONES, vox), BF16),
            pltpu.VMEM((subsets, slices, chunk), BF16),
            pltpu.VMEM((PASSES, slices, chunk), F32),
            pltpu.VMEM((1, chunk), F32),
            pltpu.VMEM((1, vox), F32),
            pltpu.VMEM((tiles, slices + ONES, chunk), BF16),
            pltpu.VMEM((PASSES, tiles, slices + ONES, chunk), BF16),
            pltpu.VMEM((PASSES, slices + ONES, rays), BF16),
            pltpu.VMEM((hops, slices, vox), BF16),
            pltpu.VMEM((hops, slices, vox), BF16),
            pltpu.VMEM((hops, slices, vox), BF16),
            pltpu.VMEM((hops, slices, vox), BF16),
            pltpu.VMEM((slices, rays), F32),
            pltpu.VMEM((subsets, slices, vox), BF16),
            dma((rays // (2 * chunk),)),
            dma((2,)),
            dma((tiles,)),
            dma((PASSES, tiles)),
            dma((tiles,)),
            dma((PASSES, tiles)),
            dma((hops, 2, chunks)),
            dma((hops, 2, chunks)),
            dma((7, chunks)),
            dma((7, chunks)),
            dma((8,)),
        ],
        compiler_params=pltpu.CompilerParams(
            collective_id=0, has_side_effects=True, vmem_limit_bytes=60 * 1024 * 1024
        ),
    )(order, mask, start, meas, system)


def body(tiles, chunks, start_volume, measured, system_values, block_pattern, subset_order):
    subsets, slices, vox = start_volume.shape
    mask = jnp.repeat(block_pattern[0].astype(F32), SIDE, axis=1)
    owners = lax.rem(subset_order + (PASSES - 1), subsets)
    same = jnp.arange(slices)[:, None, None, None] == jnp.arange(slices)[None, None, None, :]
    hit = owners[:, :, None, None] == jnp.arange(subsets)[None, None, :, None]
    pick = jnp.transpose(same & hit, (1, 0, 2, 3)).reshape(subsets * slices, subsets * slices).astype(BF16)
    gathered = sweep(tiles, chunks, subset_order, mask, start_volume, measured, system_values)
    placed = dot(pick, gathered.reshape(subsets * slices, vox), NN)
    return placed.astype(BF16).reshape(start_volume.shape)


def solution(mesh):
    placed = (
        P(None, None, "tile"),
        P("subset", None, None, None),
        P("subset", None, "tile"),
        P("subset", None, "tile"),
        P(),
    )
    return jax.shard_map(
        functools.partial(body, mesh.shape["tile"], 8),
        mesh=mesh, in_specs=placed, out_specs=P(None, None, "tile"), check_vma=False,
    )
```

```python
import functools

import jax
import jax.numpy as jnp
from jax import lax
from jax.experimental import pallas as pl
from jax.experimental.pallas import tpu as pltpu
from jax.sharding import PartitionSpec as P

MESH = pl.DeviceIdType.MESH
F32 = jnp.float32
BF16 = jnp.bfloat16
SIDE = 128
PASSES = 4
ONES = 16
NT = (((1,), (1,)), ((), ()))
NN = (((1,), (0,)), ((), ()))


def dot(a, b, dims):
    return lax.dot_general(a, b, dims, preferred_element_type=F32)


def sweep_kernel(
    tiles, order_hbm, pattern_hbm, start_hbm, meas_hbm, sys_hbm, out_hbm,
    order_ref, pattern_ref, mask_ref, a_ref, start_ref, vb_ref, meas_ref, dest_ref, rows_ref, inv_ref,
    part, recv, resid, mid_out, mid_in, hop_out, hop_in, acc, gat,
    a_sem, io_sem, rs_send, rs_recv, ag_send, ag_recv, mid_send, mid_recv, hop_send, hop_recv,
    fin_send, fin_recv, out_sem,
):
    me_s, me_t = lax.axis_index("subset"), lax.axis_index("tile")
    subsets = order_ref.shape[1]
    slices = order_ref.shape[0]
    rays, vox = a_ref.shape
    chunk = rays // tiles
    pair = 2 * chunk
    pairs = rays // pair
    chunks = hop_send.shape[1]
    width = vox // chunks

    def tile_at(d):
        return lax.rem(me_t + d, tiles)

    def subset_at(d):
        return lax.rem(me_s + d, subsets)

    def remote(src, dst, send, recv_, s, t):
        return pltpu.make_async_remote_copy(
            src_ref=src, dst_ref=dst, send_sem=send, recv_sem=recv_,
            device_id=(s, t), device_id_type=MESH,
        )

    def cols(n):
        return pl.ds(pl.multiple_of(n * width, width), width)

    def rays_of(c):
        return pl.ds(pl.multiple_of(c * chunk, chunk), chunk)

    order_copy = pltpu.make_async_copy(order_hbm, order_ref, io_sem.at[2])
    order_copy.start()
    pattern_copy = pltpu.make_async_copy(pattern_hbm.at[0], pattern_ref, io_sem.at[3])
    pattern_copy.start()
    start_copy = pltpu.make_async_copy(start_hbm, start_ref, io_sem.at[0])
    start_copy.start()
    half = lax.div(me_t, 2)

    def block_rows(i):
        return pl.ds(pl.multiple_of(lax.rem(half + i, pairs) * pair, pair), pair)

    def matrix_copy(i):
        return pltpu.make_async_copy(
            sys_hbm.at[0, block_rows(i), :], a_ref.at[block_rows(i), :], a_sem.at[i]
        )

    for i in range(pairs):
        matrix_copy(i).start()
    meas_copy = pltpu.make_async_copy(
        meas_hbm.at[0, :, :, rays_of(me_t)], meas_ref, io_sem.at[1]
    )
    meas_copy.start()

    barrier = pltpu.get_barrier_semaphore()
    for d in range(1, tiles):
        pl.semaphore_signal(barrier, inc=1, device_id=(me_s, tile_at(d)), device_id_type=MESH)
    for d in range(1, subsets):
        pl.semaphore_signal(barrier, inc=1, device_id=(subset_at(d), me_t), device_id_type=MESH)

    vb_ref[slices:, :] = jnp.ones((ONES, vox), BF16)
    resid[0, slices:, :] = jnp.ones((ONES, rays), BF16)

    def select_start(source, n):
        total = jnp.zeros((slices, width), F32)
        for f in range(subsets):
            weight = (order_ref[:, f : f + 1] == source).astype(F32)
            total += weight * start_ref[f, :, cols(n)].astype(F32)
        return total.astype(BF16)

    pattern_copy.wait()
    blocks = pattern_ref.shape[1]
    spread = lax.broadcasted_iota(jnp.int32, (blocks, vox), 1) // SIDE == lax.broadcasted_iota(
        jnp.int32, (blocks, vox), 0
    )
    mask_ref[...] = dot(
        pattern_ref[...].astype(F32).astype(BF16), spread.astype(F32).astype(BF16), NN
    )
    order_copy.wait()
    start_copy.wait()

    @pl.loop(0, chunks)
    def _(n):
        vb_ref[:slices, cols(n)] = select_start(me_s, n)

    pl.semaphore_wait(barrier, tiles - 1 + subsets - 1)

    def rs_copy(j, d, c, height):
        return remote(
            part.at[c, pl.ds(0, height), :], recv.at[j, d, pl.ds(0, height), :],
            rs_send.at[d], rs_recv.at[j, d], me_s, tile_at(d),
        )

    @pl.loop(0, pairs)
    def _(i):
        matrix_copy(i).wait()
        b = lax.rem(half + i, pairs)
        per_pair = pair // SIDE
        for q in range(per_pair):
            mask = jnp.broadcast_to(mask_ref[pl.ds(b * per_pair + q, 1), :], (16, vox)).astype(BF16)
            for u in range(SIDE // 16):
                here = pl.ds(pl.multiple_of(b * pair + q * SIDE + u * 16, 16), 16)
                a_ref[here, :] = a_ref[here, :] * mask
        p = dot(vb_ref[...], a_ref[block_rows(i), :], NT)
        sums = p[slices:, :]
        high = sums.astype(BF16)
        rest = sums - high.astype(F32)
        mid = rest.astype(BF16)
        low = (rest - mid.astype(F32)).astype(BF16)
        row = lax.broadcasted_iota(jnp.int32, sums.shape, 0)
        packed = jnp.where(
            row == 0, high.astype(F32),
            jnp.where(row == 1, mid.astype(F32), jnp.where(row == 2, low.astype(F32), 0.0)),
        ).astype(BF16)
        for h in range(2):
            c = 2 * b + h
            part[c, pl.ds(0, slices), :] = p[:slices, h * chunk : (h + 1) * chunk].astype(BF16)
            part[c, pl.ds(slices, ONES), :] = packed[:, h * chunk : (h + 1) * chunk]
            d = lax.rem(c + tiles - me_t, tiles)

            @pl.when(d != 0)
            def _():
                rs_copy(0, d, c, slices + ONES).start()

    meas_copy.wait()
    for j in range(PASSES):
        source = lax.rem(me_s + subsets - j, subsets)
        total = jnp.zeros((slices, chunk), F32)
        for f in range(subsets):
            weight = (order_ref[:, f : f + 1] == source).astype(F32)
            total += weight * meas_ref[f].astype(F32)
        dest_ref[j] = total

    def ag_copy(j, d):
        here = resid.at[j, pl.ds(0, slices), rays_of(me_t)]
        return remote(here, here, ag_send.at[d], ag_recv.at[j, d], me_s, tile_at(d))

    def ag_arrival(j, d):
        here = resid.at[j, pl.ds(0, slices), rays_of(lax.rem(me_t + tiles - d, tiles))]
        return remote(here, here, ag_send.at[d], ag_recv.at[j, d], me_s, tile_at(d))

    def hop_copy(j, n):
        return remote(
            hop_out.at[j, :, cols(n)], hop_in.at[j, :, cols(n)],
            hop_send.at[j, n], hop_recv.at[j, n], subset_at(1), me_t,
        )

    def mid_copy(j):
        return remote(
            mid_out.at[j], mid_in.at[j], mid_send.at[j], mid_recv.at[j], subset_at(1), me_t
        )

    def wide(x):
        return jnp.concatenate([x] * (width // x.shape[1]), axis=1)

    def change_so_far(j, n):
        return hop_in[j - 1, :, cols(n)].astype(F32) + wide(mid_in[j - 1].astype(F32))

    zp = me_s + 1 - 2 * lax.rem(me_s, 2)
    yp, ym, y2 = subset_at(2), subset_at(subsets - 2), subset_at(subsets // 2)
    zp_p = lax.rem(zp + 2, subsets)
    zp_m = lax.rem(zp + subsets - 2, subsets)
    zp_2 = lax.rem(zp + subsets // 2, subsets)

    def fin_copy(kind, block, n, target):
        here = gat.at[block, :, cols(n)]
        return remote(here, here, fin_send.at[kind, n], fin_recv.at[kind, n], target, me_t)

    for j in range(PASSES):
        height = slices + ONES if j == 0 else slices
        if j > 0:
            acc[...] = jnp.zeros_like(acc)
            mid_copy(j - 1).wait_recv()

            @pl.loop(0, chunks)
            def _(n):
                hop_copy(j - 1, n).wait_recv()
                volume = vb_ref[:slices, cols(n)].astype(F32) + change_so_far(j, n)
                acc[...] += dot(volume.astype(BF16), a_ref[:, cols(n)], NT)

            for c in range(tiles):
                part[c, pl.ds(0, slices), :] = acc[:, c * chunk : (c + 1) * chunk].astype(BF16)
            for d in range(1, tiles):
                rs_copy(j, d, tile_at(d), slices).start()

        if j + 1 < PASSES:
            @pl.loop(0, chunks)
            def _(n):
                vb_ref[:slices, cols(n)] = select_start(lax.rem(me_s + subsets - j - 1, subsets), n)

        total = part[me_t].astype(F32) if j == 0 else part[me_t, pl.ds(0, slices), :].astype(F32)
        for d in range(1, tiles):
            rs_copy(j, d, tile_at(d), height).wait_recv()
            total += recv[j, d, pl.ds(0, height), :].astype(F32)
        if j == 0:
            rows_ref[...] = jnp.sum(total[slices:, :], axis=0, keepdims=True)
        value = (dest_ref[j] - total[:slices, :]) / rows_ref[...]
        resid[j, pl.ds(0, slices), rays_of(me_t)] = value.astype(BF16)
        for d in range(1, tiles):
            ag_copy(j, d).start()
        for d in range(1, tiles):
            rs_copy(j, d, tile_at(d), height).wait_send()
        for d in range(1, tiles):
            ag_arrival(j, d).wait_recv()

        @pl.loop(0, chunks)
        def _(n):
            here = cols(n)
            if j == 0:
                back = dot(resid[0], a_ref[:, here], NN)
                inv = 1.0 / back[slices : slices + 1, :]
                inv_ref[:, here] = inv
                change = back[:slices, :] * inv
            else:
                back = dot(resid[j, pl.ds(0, slices), :], a_ref[:, here], NN)
                change = change_so_far(j, n) + back * inv_ref[:, here]
            if j + 1 < PASSES:
                @pl.when(n == 0)
                def _():
                    mean = jnp.sum(change, axis=1, keepdims=True) * (1.0 / width)
                    mid_out[j] = jnp.broadcast_to(mean, mid_out.shape[1:]).astype(BF16)
                    mid_copy(j).start()

                hop_out[j, :, here] = (change - wide(mid_out[j].astype(F32))).astype(BF16)
                hop_copy(j, n).start()
            else:
                gat[me_s, :, here] = (vb_ref[:slices, here].astype(F32) + change).astype(BF16)
                fin_copy(0, me_s, n, zp).start()
                fin_copy(1, me_s, n, yp).start()
                fin_copy(2, me_s, n, ym).start()

        for d in range(1, tiles):
            ag_copy(j, d).wait_send()

    @pl.loop(0, chunks)
    def _(n):
        fin_copy(1, ym, n, me_s).wait_recv()
        fin_copy(2, yp, n, me_s).wait_recv()

        @pl.when(lax.rem(n, 2) == 0)
        def _():
            fin_copy(3, ym, n, yp).start()

        @pl.when(lax.rem(n, 2) == 1)
        def _():
            fin_copy(3, yp, n, ym).start()

    @pl.loop(0, chunks)
    def _(n):
        fin_copy(0, zp, n, me_s).wait_recv()
        fin_copy(4, zp, n, yp).start()
        fin_copy(5, zp, n, ym).start()

    def out_copy(block, i):
        return pltpu.make_async_copy(gat.at[block], out_hbm.at[block], out_sem.at[i])

    for i, block in enumerate((me_s, zp, yp, ym)):
        out_copy(block, i).start()

    @pl.loop(0, chunks)
    def _(n):
        fin_copy(3, y2, n, me_s).wait_recv()
        fin_copy(6, y2, n, zp).start()

    out_copy(y2, 4).start()

    @pl.loop(0, chunks)
    def _(n):
        fin_copy(4, zp_m, n, me_s).wait_recv()
        fin_copy(5, zp_p, n, me_s).wait_recv()

    out_copy(zp_m, 5).start()
    out_copy(zp_p, 6).start()

    @pl.loop(0, chunks)
    def _(n):
        fin_copy(6, zp_2, n, me_s).wait_recv()

    out_copy(zp_2, 7).start()

    @pl.loop(0, chunks)
    def _(n):
        for kind in range(7):
            fin_copy(kind, me_s, n, zp).wait_send()
        for j in range(PASSES - 1):
            hop_copy(j, n).wait_send()

    for j in range(PASSES - 1):
        mid_copy(j).wait_send()

    for i, block in enumerate((me_s, zp, yp, ym, y2, zp_m, zp_p, zp_2)):
        out_copy(block, i).wait()


def sweep(tiles, chunks, order, pattern, start, meas, system):
    subsets, slices, vox = start.shape
    rays = system.shape[1]
    chunk = rays // tiles
    hops = PASSES - 1
    dma = pltpu.SemaphoreType.DMA
    hbm = pl.BlockSpec(memory_space=pl.ANY)
    return pl.pallas_call(
        functools.partial(sweep_kernel, tiles),
        out_shape=jax.ShapeDtypeStruct((subsets, slices, vox), BF16),
        in_specs=[hbm] * 5,
        out_specs=hbm,
        scratch_shapes=[
            pltpu.VMEM(order.shape, jnp.int32),
            pltpu.VMEM(pattern.shape[1:], jnp.int32),
            pltpu.VMEM((pattern.shape[1], vox), F32),
            pltpu.VMEM((rays, vox), BF16),
            pltpu.VMEM((subsets, slices, vox), BF16),
            pltpu.VMEM((slices + ONES, vox), BF16),
            pltpu.VMEM((subsets, slices, chunk), BF16),
            pltpu.VMEM((PASSES, slices, chunk), F32),
            pltpu.VMEM((1, chunk), F32),
            pltpu.VMEM((1, vox), F32),
            pltpu.VMEM((tiles, slices + ONES, chunk), BF16),
            pltpu.VMEM((PASSES, tiles, slices + ONES, chunk), BF16),
            pltpu.VMEM((PASSES, slices + ONES, rays), BF16),
            pltpu.VMEM((hops, slices, SIDE), BF16),
            pltpu.VMEM((hops, slices, SIDE), BF16),
            pltpu.VMEM((hops, slices, vox), BF16),
            pltpu.VMEM((hops, slices, vox), BF16),
            pltpu.VMEM((slices, rays), F32),
            pltpu.VMEM((subsets, slices, vox), BF16),
            dma((rays // (2 * chunk),)),
            dma((4,)),
            dma((tiles,)),
            dma((PASSES, tiles)),
            dma((tiles,)),
            dma((PASSES, tiles)),
            dma((hops,)),
            dma((hops,)),
            dma((hops, chunks)),
            dma((hops, chunks)),
            dma((7, chunks)),
            dma((7, chunks)),
            dma((8,)),
        ],
        compiler_params=pltpu.CompilerParams(
            collective_id=0, has_side_effects=True, vmem_limit_bytes=60 * 1024 * 1024
        ),
    )(order, pattern, start, meas, system)


def place_kernel(order_ref, gathered_ref, out_ref, pick_ref):
    fronts, slices, width = gathered_ref.shape
    half = slices // 2
    side = fronts * half

    @pl.when(pl.program_id(0) == 0)
    def _():
        column = lax.broadcasted_iota(jnp.int32, (half, side), 1)
        row = lax.broadcasted_iota(jnp.int32, (half, side), 0)
        for h in range(2):
            for f in range(fronts):
                owner = lax.rem(order_ref[h * half : (h + 1) * half, f : f + 1] + (PASSES - 1), fronts)
                hit = column == owner * half + row
                pick_ref[h, f * half : (f + 1) * half, :] = hit.astype(F32).astype(BF16)

    for h in range(2):
        rows = gathered_ref[:, h * half : (h + 1) * half, :].reshape(side, width)
        placed = dot(pick_ref[h], rows, NN).astype(BF16)
        out_ref[:, h * half : (h + 1) * half, :] = placed.reshape(fronts, half, width)


def place(order, gathered, steps):
    fronts, slices, vox = gathered.shape
    block = pl.BlockSpec((fronts, slices, vox // steps), lambda n: (0, 0, n))
    side = fronts * slices // 2
    return pl.pallas_call(
        place_kernel,
        out_shape=jax.ShapeDtypeStruct(gathered.shape, BF16),
        grid=(steps,),
        in_specs=[pl.BlockSpec(order.shape, lambda n: (0, 0)), block],
        out_specs=block,
        scratch_shapes=[pltpu.VMEM((2, side, side), BF16)],
    )(order, gathered)


def body(tiles, chunks, start_volume, measured, system_values, block_pattern, subset_order):
    gathered = sweep(
        tiles, chunks, subset_order, block_pattern, start_volume, measured, system_values
    )
    return place(subset_order, gathered, 8)


def solution(mesh):
    placed = (
        P(None, None, "tile"),
        P("subset", None, None, None),
        P("subset", None, "tile"),
        P("subset", None, "tile"),
        P(),
    )
    return jax.shard_map(
        functools.partial(body, mesh.shape["tile"], 8),
        mesh=mesh, in_specs=placed, out_specs=P(None, None, "tile"), check_vma=False,
    )
```

```python
import functools

import jax
import jax.numpy as jnp
from jax import lax
from jax.experimental import pallas as pl
from jax.experimental.pallas import tpu as pltpu
from jax.sharding import PartitionSpec as P

MESH = pl.DeviceIdType.MESH
F32 = jnp.float32
BF16 = jnp.bfloat16
SIDE = 128
PASSES = 4
ONES = 16
NT = (((1,), (1,)), ((), ()))
NN = (((1,), (0,)), ((), ()))


TN = (((0,), (0,)), ((), ()))
LATE = 3


def bit(x, k):
    return lax.rem(lax.div(x, 2**k), 2)


def flip(x, d):
    for k in range(d.bit_length()):
        if d >> k & 1:
            x = x + 2**k * (1 - 2 * bit(x, k))
    return x


def differ(x, y, bits):
    return sum(2**k * lax.rem(bit(x, k) + bit(y, k), 2) for k in range(bits))


def dot(a, b, dims):
    return lax.dot_general(a, b, dims, preferred_element_type=F32)


def sweep_kernel(
    tiles, order_hbm, pattern_hbm, start_hbm, meas_hbm, sys_hbm, out_hbm,
    turned_ref, order_ref, pick_ref, pattern_ref, mask_ref, a_ref, start_ref, vb_ref, meas_ref, dest_ref, rows_ref, inv_ref,
    part, recv, resid, mid_out, mid_in, hop_out, hop_in, acc, gat,
    a_sem, io_sem, rs_send, rs_recv, ag_send, ag_recv, mid_send, mid_recv, hop_send, hop_recv,
    fin_send, fin_recv, out_sem,
):
    me_s, me_t = lax.axis_index("subset"), lax.axis_index("tile")
    subsets = order_ref.shape[1]
    slices = order_ref.shape[0]
    bits = (tiles - 1).bit_length()
    partners = sorted(range(1, tiles), key=lambda d: -(4 * (d >> 3) + 2 * (d >> 2 & 1) * (1 - (d >> 1 & 1)) + (d >> 1 & 1)))
    rays, vox = a_ref.shape
    chunk = rays // tiles
    pair = 2 * chunk
    pairs = rays // pair
    chunks = hop_send.shape[1]
    width = vox // chunks

    def tile_at(d):
        return flip(me_t, d)

    def subset_at(d):
        return lax.rem(me_s + d, subsets)

    def remote(src, dst, send, recv_, s, t):
        return pltpu.make_async_remote_copy(
            src_ref=src, dst_ref=dst, send_sem=send, recv_sem=recv_,
            device_id=(s, t), device_id_type=MESH,
        )

    def cols(n):
        return pl.ds(pl.multiple_of(n * width, width), width)

    def rays_of(c):
        return pl.ds(pl.multiple_of(c * chunk, chunk), chunk)

    order_copy = pltpu.make_async_copy(order_hbm, turned_ref, io_sem.at[2])
    order_copy.start()
    pattern_copy = pltpu.make_async_copy(pattern_hbm.at[0], pattern_ref, io_sem.at[3])
    pattern_copy.start()
    start_copy = pltpu.make_async_copy(start_hbm, start_ref, io_sem.at[0])
    start_copy.start()
    half = lax.div(me_t, 2)

    def pair_at(i):
        return flip(differ(half, i, bits), max(pairs - 2, 0))

    def block_rows(i):
        return pl.ds(pl.multiple_of(pair_at(i) * pair, pair), pair)

    def matrix_copy(i):
        return pltpu.make_async_copy(
            sys_hbm.at[0, block_rows(i), :], a_ref.at[block_rows(i), :], a_sem.at[i]
        )

    for i in range(pairs):
        matrix_copy(i).start()
    meas_copy = pltpu.make_async_copy(
        meas_hbm.at[0, :, :, rays_of(me_t)], meas_ref, io_sem.at[1]
    )
    meas_copy.start()

    barrier = pltpu.get_barrier_semaphore()
    for d in range(1, tiles):
        pl.semaphore_signal(barrier, inc=1, device_id=(me_s, tile_at(d)), device_id_type=MESH)
    for d in range(1, subsets):
        pl.semaphore_signal(barrier, inc=1, device_id=(subset_at(d), me_t), device_id_type=MESH)

    vb_ref[slices:, :] = jnp.ones((ONES, vox), BF16)
    resid[0, slices:, :] = jnp.ones((ONES, rays), BF16)

    def wide(x):
        return jnp.concatenate([x] * (width // x.shape[1]), axis=1)

    def hits(source):
        return [
            jnp.broadcast_to((order_ref[:, f : f + 1] == source).astype(F32), (slices, SIDE)).astype(BF16)
            for f in range(subsets)
        ]

    def select_start(source):
        weights = hits(source)

        @pl.loop(0, chunks)
        def _(n):
            total = wide(weights[0]) * start_ref[0, :, cols(n)]
            for f in range(1, subsets):
                total += wide(weights[f]) * start_ref[f, :, cols(n)]
            vb_ref[:slices, cols(n)] = total

    pattern_copy.wait()
    blocks = pattern_ref.shape[1]
    spread = lax.broadcasted_iota(jnp.int32, (blocks, vox), 1) // SIDE == lax.broadcasted_iota(
        jnp.int32, (blocks, vox), 0
    )
    mask_ref[...] = dot(
        pattern_ref[...].astype(F32).astype(BF16), spread.astype(F32).astype(BF16), NN
    )
    order_copy.wait()
    same = lax.broadcasted_iota(jnp.int32, (subsets, subsets), 0) == lax.broadcasted_iota(
        jnp.int32, (subsets, subsets), 1
    )
    order_ref[...] = dot(
        turned_ref[...].astype(F32).astype(BF16), same.astype(F32).astype(BF16), TN
    ).astype(jnp.int32)
    start_copy.wait()
    select_start(me_s)

    pl.semaphore_wait(barrier, tiles - 1 + subsets - 1)

    def rs_copy(j, d, c, height):
        return remote(
            part.at[c, pl.ds(0, height), :], recv.at[j, d, pl.ds(0, height), :],
            rs_send.at[d], rs_recv.at[j, d], me_s, c,
        )

    @pl.loop(0, pairs)
    def _(i):
        matrix_copy(i).wait()
        b = pair_at(i)
        per_pair = pair // SIDE
        piece = min(512, vox)
        p = jnp.zeros((slices + ONES, pair), F32)
        for k in range(0, vox, piece):
            parts = []
            for q in range(per_pair):
                mask = jnp.broadcast_to(mask_ref[pl.ds(b * per_pair + q, 1), k : k + piece], (16, piece)).astype(BF16)
                here = pl.ds(pl.multiple_of(b * pair + q * SIDE, SIDE), SIDE)
                masked = a_ref[here, k : k + piece] * jnp.concatenate([mask] * (SIDE // 16), axis=0)
                a_ref[here, k : k + piece] = masked
                parts.append(masked)
            p += dot(vb_ref[:, k : k + piece], jnp.concatenate(parts, axis=0), NT)
        sums = p[slices:, :]
        high = sums.astype(BF16)
        rest = sums - high.astype(F32)
        mid = rest.astype(BF16)
        low = (rest - mid.astype(F32)).astype(BF16)
        row = lax.broadcasted_iota(jnp.int32, sums.shape, 0)
        packed = jnp.where(
            row == 0, high.astype(F32),
            jnp.where(row == 1, mid.astype(F32), jnp.where(row == 2, low.astype(F32), 0.0)),
        ).astype(BF16)
        for h in range(2):
            c = 2 * b + h
            part[c, pl.ds(0, slices), :] = p[:slices, h * chunk : (h + 1) * chunk].astype(BF16)
            part[c, pl.ds(slices, ONES), :] = packed[:, h * chunk : (h + 1) * chunk]
            d = differ(c, me_t, bits)

            @pl.when(d != 0)
            def _():
                rs_copy(0, d, c, slices + ONES).start()

    half_slices = slices // 2
    side = subsets * half_slices
    column = lax.broadcasted_iota(jnp.int32, (half_slices, side), 1)
    row = lax.broadcasted_iota(jnp.int32, (half_slices, side), 0)
    for h in range(2):
        for f in range(subsets):
            last = lax.rem(order_ref[h * half_slices : (h + 1) * half_slices, f : f + 1] + (PASSES - 1), subsets)
            hit = column == last * half_slices + row
            pick_ref[h, f * half_slices : (f + 1) * half_slices, :] = hit.astype(F32).astype(BF16)

    meas_copy.wait()
    for j in range(PASSES):
        source = lax.rem(me_s + subsets - j, subsets)
        total = jnp.zeros((slices, chunk), F32)
        for f in range(subsets):
            weight = (order_ref[:, f : f + 1] == source).astype(F32)
            total += weight * meas_ref[f].astype(F32)
        dest_ref[j] = total

    def ag_copy(j, d):
        here = resid.at[j, pl.ds(0, slices), rays_of(me_t)]
        return remote(here, here, ag_send.at[d], ag_recv.at[j, d], me_s, tile_at(d))

    def ag_arrival(j, d):
        here = resid.at[j, pl.ds(0, slices), rays_of(tile_at(d))]
        return remote(here, here, ag_send.at[d], ag_recv.at[j, d], me_s, tile_at(d))

    def hop_copy(j, n):
        return remote(
            hop_out.at[j, :, cols(n)], hop_in.at[j, :, cols(n)],
            hop_send.at[j, n], hop_recv.at[j, n], subset_at(1), me_t,
        )

    def mid_copy(j):
        return remote(
            mid_out.at[j], mid_in.at[j], mid_send.at[j], mid_recv.at[j], subset_at(1), me_t
        )

    def change_so_far(j, n):
        return hop_in[j - 1, :, cols(n)].astype(F32) + wide(mid_in[j - 1].astype(F32))

    zp = me_s + 1 - 2 * lax.rem(me_s, 2)
    yp, ym, y2 = subset_at(2), subset_at(subsets - 2), subset_at(subsets // 2)
    zp_p = lax.rem(zp + 2, subsets)
    zp_m = lax.rem(zp + subsets - 2, subsets)
    zp_2 = lax.rem(zp + subsets // 2, subsets)

    def fin_copy(kind, block, n, target):
        here = gat.at[block, :, cols(n)]
        return remote(here, here, fin_send.at[kind, n], fin_recv.at[kind, n], target, me_t)

    for j in range(PASSES):
        height = slices + ONES if j == 0 else slices
        if j > 0:
            acc[...] = jnp.zeros_like(acc)
            mid_copy(j - 1).wait_recv()

            @pl.loop(0, chunks)
            def _(n):
                hop_copy(j - 1, n).wait_recv()
                volume = vb_ref[:slices, cols(n)].astype(F32) + change_so_far(j, n)
                acc[...] += dot(volume.astype(BF16), a_ref[:, cols(n)], NT)

            for c in range(tiles):
                part[c, pl.ds(0, slices), :] = acc[:, c * chunk : (c + 1) * chunk].astype(BF16)
            for d in partners:
                rs_copy(j, d, tile_at(d), slices).start()

        if j + 1 < PASSES:
            select_start(lax.rem(me_s + subsets - j - 1, subsets))

        total = part[me_t].astype(F32) if j == 0 else part[me_t, pl.ds(0, slices), :].astype(F32)
        for d in reversed(partners):
            rs_copy(j, d, tile_at(d), height).wait_recv()
            total += recv[j, d, pl.ds(0, height), :].astype(F32)
        if j == 0:
            rows_ref[...] = jnp.sum(total[slices:, :], axis=0, keepdims=True)
        value = (dest_ref[j] - total[:slices, :]) / rows_ref[...]
        resid[j, pl.ds(0, slices), rays_of(me_t)] = value.astype(BF16)
        for d in partners:
            ag_copy(j, d).start()
        for d in range(1, tiles):
            rs_copy(j, d, tile_at(d), height).wait_send()
        for d in range(1, tiles):
            ag_arrival(j, d).wait_recv()

        @pl.loop(0, chunks)
        def _(n):
            here = cols(n)
            if j == 0:
                back = dot(resid[0], a_ref[:, here], NN)
                inv = 1.0 / back[slices : slices + 1, :]
                inv_ref[:, here] = inv
                change = back[:slices, :] * inv
            else:
                back = dot(resid[j, pl.ds(0, slices), :], a_ref[:, here], NN)
                change = change_so_far(j, n) + back * inv_ref[:, here]
            if j + 1 < PASSES:
                @pl.when(n == 0)
                def _():
                    mean = jnp.sum(change, axis=1, keepdims=True) * (1.0 / width)
                    mid_out[j] = jnp.broadcast_to(mean, mid_out.shape[1:]).astype(BF16)
                    mid_copy(j).start()

                hop_out[j, :, here] = (change - wide(mid_out[j].astype(F32))).astype(BF16)
                hop_copy(j, n).start()
            else:
                gat[me_s, :, here] = (vb_ref[:slices, here].astype(F32) + change).astype(BF16)
                fin_copy(0, me_s, n, zp).start()
                fin_copy(1, me_s, n, yp).start()
                fin_copy(2, me_s, n, ym).start()

        for d in range(1, tiles):
            ag_copy(j, d).wait_send()

    late = min(LATE, chunks - 1)

    @pl.loop(0, chunks)
    def _(n):
        fin_copy(1, ym, n, me_s).wait_recv()
        fin_copy(2, yp, n, me_s).wait_recv()

        @pl.when(lax.rem(n, 2) == 0)
        def _():
            fin_copy(3, ym, n, yp).start()

        @pl.when(lax.rem(n, 2) == 1)
        def _():
            fin_copy(3, yp, n, ym).start()

        @pl.when(n < late)
        def _():
            fin_copy(7, ym, n, zp).start()
            fin_copy(8, yp, n, zp).start()

    @pl.loop(0, chunks)
    def _(n):
        fin_copy(0, zp, n, me_s).wait_recv()

        @pl.when(n >= late)
        def _():
            fin_copy(4, zp, n, yp).start()
            fin_copy(5, zp, n, ym).start()

    @pl.loop(0, chunks)
    def _(n):
        fin_copy(3, y2, n, me_s).wait_recv()
        fin_copy(6, y2, n, zp).start()

    def out_copy(n):
        return pltpu.make_async_copy(start_ref.at[:, :, cols(n)], out_hbm.at[:, :, cols(n)], out_sem.at[n])

    @pl.loop(0, chunks)
    def _(n):
        @pl.when(n < late)
        def _():
            fin_copy(7, zp_m, n, me_s).wait_recv()
            fin_copy(8, zp_p, n, me_s).wait_recv()

        @pl.when(n >= late)
        def _():
            fin_copy(4, zp_m, n, me_s).wait_recv()
            fin_copy(5, zp_p, n, me_s).wait_recv()

        fin_copy(6, zp_2, n, me_s).wait_recv()
        for h in range(2):
            there = pl.ds(h * half_slices, half_slices)
            rows = gat[:, there, cols(n)].reshape(side, width)
            placed = dot(pick_ref[h], rows, NN).astype(BF16)
            start_ref[:, there, cols(n)] = placed.reshape(subsets, half_slices, width)
        out_copy(n).start()

    @pl.loop(0, chunks)
    def _(n):
        for kind in (0, 1, 2, 3, 6):
            fin_copy(kind, me_s, n, zp).wait_send()

        @pl.when(n < late)
        def _():
            fin_copy(7, me_s, n, zp).wait_send()
            fin_copy(8, me_s, n, zp).wait_send()

        @pl.when(n >= late)
        def _():
            fin_copy(4, me_s, n, zp).wait_send()
            fin_copy(5, me_s, n, zp).wait_send()

        for j in range(PASSES - 1):
            hop_copy(j, n).wait_send()
        out_copy(n).wait()

    for j in range(PASSES - 1):
        mid_copy(j).wait_send()


def sweep(tiles, chunks, order, pattern, start, meas, system):
    subsets, slices, vox = start.shape
    rays = system.shape[1]
    chunk = rays // tiles
    hops = PASSES - 1
    dma = pltpu.SemaphoreType.DMA
    hbm = pl.BlockSpec(memory_space=pl.ANY)
    return pl.pallas_call(
        functools.partial(sweep_kernel, tiles),
        out_shape=jax.ShapeDtypeStruct((subsets, slices, vox), BF16),
        in_specs=[hbm] * 5,
        out_specs=hbm,
        scratch_shapes=[
            pltpu.VMEM(order.shape, jnp.int32),
            pltpu.VMEM(order.shape[::-1], jnp.int32),
            pltpu.VMEM((2, subsets * slices // 2, subsets * slices // 2), BF16),
            pltpu.VMEM(pattern.shape[1:], jnp.int32),
            pltpu.VMEM((pattern.shape[1], vox), F32),
            pltpu.VMEM((rays, vox), BF16),
            pltpu.VMEM((subsets, slices, vox), BF16),
            pltpu.VMEM((slices + ONES, vox), BF16),
            pltpu.VMEM((subsets, slices, chunk), BF16),
            pltpu.VMEM((PASSES, slices, chunk), F32),
            pltpu.VMEM((1, chunk), F32),
            pltpu.VMEM((1, vox), F32),
            pltpu.VMEM((tiles, slices + ONES, chunk), BF16),
            pltpu.VMEM((PASSES, tiles, slices + ONES, chunk), BF16),
            pltpu.VMEM((PASSES, slices + ONES, rays), BF16),
            pltpu.VMEM((hops, slices, SIDE), BF16),
            pltpu.VMEM((hops, slices, SIDE), BF16),
            pltpu.VMEM((hops, slices, vox), BF16),
            pltpu.VMEM((hops, slices, vox), BF16),
            pltpu.VMEM((slices, rays), F32),
            pltpu.VMEM((subsets, slices, vox), BF16),
            dma((rays // (2 * chunk),)),
            dma((4,)),
            dma((tiles,)),
            dma((PASSES, tiles)),
            dma((tiles,)),
            dma((PASSES, tiles)),
            dma((hops,)),
            dma((hops,)),
            dma((hops, chunks)),
            dma((hops, chunks)),
            dma((9, chunks)),
            dma((9, chunks)),
            dma((chunks,)),
        ],
        compiler_params=pltpu.CompilerParams(
            collective_id=0, has_side_effects=True, vmem_limit_bytes=60 * 1024 * 1024
        ),
    )(order, pattern, start, meas, system)


def body(tiles, chunks, start_volume, measured, system_values, block_pattern, subset_order):
    return sweep(
        tiles, chunks, jnp.transpose(subset_order), block_pattern, start_volume, measured, system_values
    )


def solution(mesh):
    placed = (
        P(None, None, "tile"),
        P("subset", None, None, None),
        P("subset", None, "tile"),
        P("subset", None, "tile"),
        P(),
    )
    return jax.shard_map(
        functools.partial(body, mesh.shape["tile"], 16),
        mesh=mesh, in_specs=placed, out_specs=P(None, None, "tile"), check_vma=False,
    )
```

```python
import functools

import jax
import jax.numpy as jnp
from jax import lax
from jax.experimental import pallas as pl
from jax.experimental.pallas import tpu as pltpu
from jax.sharding import PartitionSpec as P

MESH = pl.DeviceIdType.MESH
F32 = jnp.float32
BF16 = jnp.bfloat16
SIDE = 128
PASSES = 4
ONES = 16
NT = (((1,), (1,)), ((), ()))
NN = (((1,), (0,)), ((), ()))


TN = (((0,), (0,)), ((), ()))
LATE = 3
GROUP = 4
PIECE = 512
VMEM_LIMIT = 44 * 1024 * 1024


def bit(x, k):
    return lax.rem(lax.div(x, 2**k), 2)


def flip(x, d):
    for k in range(d.bit_length()):
        if d >> k & 1:
            x = x + 2**k * (1 - 2 * bit(x, k))
    return x


def differ(x, y, bits):
    return sum(2**k * lax.rem(bit(x, k) + bit(y, k), 2) for k in range(bits))


def dot(a, b, dims):
    return lax.dot_general(a, b, dims, preferred_element_type=F32)


def sweep_kernel(
    tiles, order_hbm, pattern_hbm, start_hbm, meas_hbm, sys_hbm, out_ref,
    turned_ref, order_ref, pick_ref, pattern_ref, mask_ref, a_ref, start_ref, vb_ref, meas_ref, dest_ref, rows_ref, inv_ref,
    part, recv, resid, mid_out, mid_in, hop_out, hop_in, acc, gat,
    a_sem, io_sem, rs_send, rs_recv, ag_send, ag_recv, mid_send, mid_recv, hop_send, hop_recv,
    fin_send, fin_recv,
):
    me_s, me_t = lax.axis_index("subset"), lax.axis_index("tile")
    subsets = order_ref.shape[1]
    slices = order_ref.shape[0]
    bits = (tiles - 1).bit_length()
    partners = sorted(range(1, tiles), key=lambda d: -(4 * (d >> 3) + 2 * (d >> 2 & 1) * (1 - (d >> 1 & 1)) + (d >> 1 & 1)))
    rays, vox = a_ref.shape
    chunk = rays // tiles
    pair = GROUP * chunk
    pairs = rays // pair
    chunks = hop_send.shape[1]
    width = vox // chunks

    chips = [d for d in partners if d % 2 == 0]
    others = [d + 1 for d in chips] + [1]

    def tile_at(d):
        return flip(me_t, d)

    def subset_at(d):
        return lax.rem(me_s + d, subsets)

    def remote(src, dst, send, recv_, s, t):
        return pltpu.make_async_remote_copy(
            src_ref=src, dst_ref=dst, send_sem=send, recv_sem=recv_,
            device_id=(s, t), device_id_type=MESH,
        )

    def cols(n):
        return pl.ds(pl.multiple_of(n * width, width), width)

    def rays_of(c):
        return pl.ds(pl.multiple_of(c * chunk, chunk), chunk)

    order_copy = pltpu.make_async_copy(order_hbm, turned_ref, io_sem.at[2])
    order_copy.start()
    pattern_copy = pltpu.make_async_copy(pattern_hbm.at[0], pattern_ref, io_sem.at[3])
    pattern_copy.start()
    start_copy = pltpu.make_async_copy(start_hbm, start_ref, io_sem.at[0])
    start_copy.start()
    half = lax.div(me_t, GROUP)

    def pair_at(i):
        return flip(differ(half, i, bits), max(pairs - 2, 0))

    def block_rows(i):
        return pl.ds(pl.multiple_of(pair_at(i) * pair, pair), pair)

    def matrix_copy(i):
        return pltpu.make_async_copy(
            sys_hbm.at[0, block_rows(i), :], a_ref.at[block_rows(i), :], a_sem.at[i]
        )

    for i in range(pairs):
        matrix_copy(i).start()
    meas_copy = pltpu.make_async_copy(
        meas_hbm.at[0, :, :, rays_of(me_t)], meas_ref, io_sem.at[1]
    )
    meas_copy.start()

    barrier = pltpu.get_barrier_semaphore()
    for d in range(1, tiles):
        pl.semaphore_signal(barrier, inc=1, device_id=(me_s, tile_at(d)), device_id_type=MESH)
    for d in range(1, subsets):
        pl.semaphore_signal(barrier, inc=1, device_id=(subset_at(d), me_t), device_id_type=MESH)

    vb_ref[slices:, :] = jnp.ones((ONES, vox), BF16)
    resid[0, slices:, :] = jnp.ones((ONES, rays), BF16)

    def wide(x):
        return jnp.concatenate([x] * (width // x.shape[1]), axis=1)

    def hits(source):
        return [
            jnp.broadcast_to((order_ref[:, f : f + 1] == source).astype(F32), (slices, SIDE)).astype(BF16)
            for f in range(subsets)
        ]

    def select_start(source):
        weights = hits(source)

        @pl.loop(0, chunks)
        def _(n):
            total = wide(weights[0]) * start_ref[0, :, cols(n)]
            for f in range(1, subsets):
                total += wide(weights[f]) * start_ref[f, :, cols(n)]
            vb_ref[:slices, cols(n)] = total

    pattern_copy.wait()
    blocks = pattern_ref.shape[1]
    spread = lax.broadcasted_iota(jnp.int32, (blocks, vox), 1) // SIDE == lax.broadcasted_iota(
        jnp.int32, (blocks, vox), 0
    )
    mask_ref[...] = dot(
        pattern_ref[...].astype(F32).astype(BF16), spread.astype(F32).astype(BF16), NN
    )
    order_copy.wait()
    same = lax.broadcasted_iota(jnp.int32, (subsets, subsets), 0) == lax.broadcasted_iota(
        jnp.int32, (subsets, subsets), 1
    )
    order_ref[...] = dot(
        turned_ref[...].astype(F32).astype(BF16), same.astype(F32).astype(BF16), TN
    ).astype(jnp.int32)
    start_copy.wait()
    select_start(me_s)

    pl.semaphore_wait(barrier, tiles - 1 + subsets - 1)

    def rs_copy(j, d, c, height, block=None):
        block = c if block is None else block
        return remote(
            part.at[block, pl.ds(0, height), :], recv.at[j, d, pl.ds(0, height), :],
            rs_send.at[d], rs_recv.at[j, d], me_s, c,
        )

    @pl.loop(0, pairs)
    def _(i):
        matrix_copy(i).wait()
        b = pair_at(i)
        per_pair = pair // SIDE
        piece = min(PIECE, vox)
        p = jnp.zeros((slices + ONES, pair), F32)
        for k in range(0, vox, piece):
            parts = []
            for q in range(per_pair):
                mask = jnp.broadcast_to(mask_ref[pl.ds(b * per_pair + q, 1), k : k + piece], (16, piece)).astype(BF16)
                here = pl.ds(pl.multiple_of(b * pair + q * SIDE, SIDE), SIDE)
                masked = a_ref[here, k : k + piece] * jnp.concatenate([mask] * (SIDE // 16), axis=0)
                a_ref[here, k : k + piece] = masked
                parts.append(masked)
            p += dot(vb_ref[:, k : k + piece], jnp.concatenate(parts, axis=0), NT)
        sums = p[slices:, :]
        high = sums.astype(BF16)
        rest = sums - high.astype(F32)
        mid = rest.astype(BF16)
        low = (rest - mid.astype(F32)).astype(BF16)
        row = lax.broadcasted_iota(jnp.int32, sums.shape, 0)
        packed = jnp.where(
            row == 0, high.astype(F32),
            jnp.where(row == 1, mid.astype(F32), jnp.where(row == 2, low.astype(F32), 0.0)),
        ).astype(BF16)
        for h in range(GROUP):
            c = GROUP * b + h
            part[c, pl.ds(0, slices), :] = p[:slices, h * chunk : (h + 1) * chunk].astype(BF16)
            part[c, pl.ds(slices, ONES), :] = packed[:, h * chunk : (h + 1) * chunk]
            d = differ(c, me_t, bits)

            @pl.when(d != 0)
            def _():
                rs_copy(0, d, c, slices + ONES).start()

    half_slices = slices // 2
    side = subsets * half_slices
    column = lax.broadcasted_iota(jnp.int32, (half_slices, side), 1)
    row = lax.broadcasted_iota(jnp.int32, (half_slices, side), 0)
    for h in range(2):
        for f in range(subsets):
            last = lax.rem(order_ref[h * half_slices : (h + 1) * half_slices, f : f + 1] + (PASSES - 1), subsets)
            hit = column == last * half_slices + row
            pick_ref[h, f * half_slices : (f + 1) * half_slices, :] = hit.astype(F32).astype(BF16)

    meas_copy.wait()
    for j in range(PASSES):
        source = lax.rem(me_s + subsets - j, subsets)
        total = jnp.zeros((slices, chunk), F32)
        for f in range(subsets):
            weight = (order_ref[:, f : f + 1] == source).astype(F32)
            total += weight * meas_ref[f].astype(F32)
        dest_ref[j] = total

    def ag_copy(j, d):
        here = resid.at[j, pl.ds(0, slices), rays_of(me_t)]
        return remote(here, here, ag_send.at[d], ag_recv.at[j, d], me_s, tile_at(d))

    def ag_arrival(j, d):
        here = resid.at[j, pl.ds(0, slices), rays_of(tile_at(d))]
        return remote(here, here, ag_send.at[d], ag_recv.at[j, d], me_s, tile_at(d))

    def hop_copy(j, n):
        return remote(
            hop_out.at[j, :, cols(n)], hop_in.at[j, :, cols(n)],
            hop_send.at[j, n], hop_recv.at[j, n], subset_at(1), me_t,
        )

    def mid_copy(j):
        return remote(
            mid_out.at[j], mid_in.at[j], mid_send.at[j], mid_recv.at[j], subset_at(1), me_t
        )

    def change_so_far(j, n):
        return hop_in[j - 1, :, cols(n)].astype(F32) + wide(mid_in[j - 1].astype(F32))

    zp = me_s + 1 - 2 * lax.rem(me_s, 2)
    yp, ym, y2 = subset_at(2), subset_at(subsets - 2), subset_at(subsets // 2)
    zp_p = lax.rem(zp + 2, subsets)
    zp_m = lax.rem(zp + subsets - 2, subsets)
    zp_2 = lax.rem(zp + subsets // 2, subsets)

    def fin_copy(kind, block, n, target):
        here = gat.at[block, :, cols(n)]
        return remote(here, here, fin_send.at[kind, n], fin_recv.at[kind, n], target, me_t)

    for j in range(PASSES):
        height = slices + ONES if j == 0 else slices
        if j > 0:
            acc[...] = jnp.zeros_like(acc)
            mid_copy(j - 1).wait_recv()

            @pl.loop(0, chunks)
            def _(n):
                hop_copy(j - 1, n).wait_recv()
                volume = vb_ref[:slices, cols(n)].astype(F32) + change_so_far(j, n)
                acc[...] += dot(volume.astype(BF16), a_ref[:, cols(n)], NT)

            for d in others:
                part[tile_at(d), pl.ds(0, slices), :] = acc[:, rays_of(tile_at(d))].astype(BF16)
                rs_copy(j, d, tile_at(1), slices, tile_at(d)).start()
            for d in chips:
                rs_copy(j, d + 1, tile_at(1), slices).wait_recv()
                both = acc[:, rays_of(tile_at(d))] + recv[j, d + 1, pl.ds(0, slices), :].astype(F32)
                part[tile_at(d), pl.ds(0, slices), :] = both.astype(BF16)
                rs_copy(j, d, tile_at(d), slices).start()

        if j + 1 < PASSES:
            select_start(lax.rem(me_s + subsets - j - 1, subsets))

        if j == 0:
            total = part[me_t].astype(F32)
        else:
            rs_copy(j, 1, tile_at(1), slices).wait_recv()
            total = acc[:, rays_of(me_t)] + recv[j, 1, pl.ds(0, slices), :].astype(F32)
        for d in reversed(partners if j == 0 else chips):
            rs_copy(j, d, tile_at(d), height).wait_recv()
            total += recv[j, d, pl.ds(0, height), :].astype(F32)
        if j == 0:
            rows_ref[...] = jnp.sum(total[slices:, :], axis=0, keepdims=True)
        value = (dest_ref[j] - total[:slices, :]) / rows_ref[...]
        resid[j, pl.ds(0, slices), rays_of(me_t)] = value.astype(BF16)
        for d in partners:
            ag_copy(j, d).start()
        for d in range(1, tiles):
            rs_copy(j, d, tile_at(d), height).wait_send()
        for d in range(1, tiles):
            ag_arrival(j, d).wait_recv()

        @pl.loop(0, chunks)
        def _(n):
            here = cols(n)
            if j == 0:
                back = dot(resid[0], a_ref[:, here], NN)
                inv = 1.0 / back[slices : slices + 1, :]
                inv_ref[:, here] = inv
                change = back[:slices, :] * inv
            else:
                back = dot(resid[j, pl.ds(0, slices), :], a_ref[:, here], NN)
                change = change_so_far(j, n) + back * inv_ref[:, here]
            if j + 1 < PASSES:
                @pl.when(n == 0)
                def _():
                    mean = jnp.sum(change, axis=1, keepdims=True) * (1.0 / width)
                    mid_out[j] = jnp.broadcast_to(mean, mid_out.shape[1:]).astype(BF16)
                    mid_copy(j).start()

                hop_out[j, :, here] = (change - wide(mid_out[j].astype(F32))).astype(BF16)
                hop_copy(j, n).start()
            else:
                gat[me_s, :, here] = (vb_ref[:slices, here].astype(F32) + change).astype(BF16)
                fin_copy(0, me_s, n, zp).start()
                fin_copy(1, me_s, n, yp).start()
                fin_copy(2, me_s, n, ym).start()

        for d in range(1, tiles):
            ag_copy(j, d).wait_send()

    late = min(LATE, chunks - 1)

    @pl.loop(0, chunks)
    def _(n):
        fin_copy(1, ym, n, me_s).wait_recv()
        fin_copy(2, yp, n, me_s).wait_recv()

        @pl.when(lax.rem(n, 2) == 0)
        def _():
            fin_copy(3, ym, n, yp).start()

        @pl.when(lax.rem(n, 2) == 1)
        def _():
            fin_copy(3, yp, n, ym).start()

        @pl.when(n < late)
        def _():
            fin_copy(7, ym, n, zp).start()
            fin_copy(8, yp, n, zp).start()

    @pl.loop(0, chunks)
    def _(n):
        fin_copy(0, zp, n, me_s).wait_recv()

        @pl.when(n >= late)
        def _():
            fin_copy(4, zp, n, yp).start()
            fin_copy(5, zp, n, ym).start()

    @pl.loop(0, chunks)
    def _(n):
        fin_copy(3, y2, n, me_s).wait_recv()
        fin_copy(6, y2, n, zp).start()

    @pl.loop(0, chunks)
    def _(n):
        @pl.when(n < late)
        def _():
            fin_copy(7, zp_m, n, me_s).wait_recv()
            fin_copy(8, zp_p, n, me_s).wait_recv()

        @pl.when(n >= late)
        def _():
            fin_copy(4, zp_m, n, me_s).wait_recv()
            fin_copy(5, zp_p, n, me_s).wait_recv()

        fin_copy(6, zp_2, n, me_s).wait_recv()
        for h in range(2):
            there = pl.ds(h * half_slices, half_slices)
            rows = gat[:, there, cols(n)].reshape(side, width)
            placed = dot(pick_ref[h], rows, NN).astype(BF16)
            out_ref[:, there, cols(n)] = placed.reshape(subsets, half_slices, width)

    @pl.loop(0, chunks)
    def _(n):
        for kind in (0, 1, 2, 3, 6):
            fin_copy(kind, me_s, n, zp).wait_send()

        @pl.when(n < late)
        def _():
            fin_copy(7, me_s, n, zp).wait_send()
            fin_copy(8, me_s, n, zp).wait_send()

        @pl.when(n >= late)
        def _():
            fin_copy(4, me_s, n, zp).wait_send()
            fin_copy(5, me_s, n, zp).wait_send()

        for j in range(PASSES - 1):
            hop_copy(j, n).wait_send()

    for j in range(PASSES - 1):
        mid_copy(j).wait_send()


def sweep(tiles, chunks, order, pattern, start, meas, system):
    subsets, slices, vox = start.shape
    rays = system.shape[1]
    chunk = rays // tiles
    hops = PASSES - 1
    dma = pltpu.SemaphoreType.DMA
    hbm = pl.BlockSpec(memory_space=pltpu.HBM)
    return pl.pallas_call(
        functools.partial(sweep_kernel, tiles),
        out_shape=jax.ShapeDtypeStruct((subsets, slices, vox), BF16),
        in_specs=[hbm] * 5,
        out_specs=pl.BlockSpec(memory_space=pltpu.VMEM),
        scratch_shapes=[
            pltpu.VMEM(order.shape, jnp.int32),
            pltpu.VMEM(order.shape[::-1], jnp.int32),
            pltpu.VMEM((2, subsets * slices // 2, subsets * slices // 2), BF16),
            pltpu.VMEM(pattern.shape[1:], jnp.int32),
            pltpu.VMEM((pattern.shape[1], vox), F32),
            pltpu.VMEM((rays, vox), BF16),
            pltpu.VMEM((subsets, slices, vox), BF16),
            pltpu.VMEM((slices + ONES, vox), BF16),
            pltpu.VMEM((subsets, slices, chunk), BF16),
            pltpu.VMEM((PASSES, slices, chunk), F32),
            pltpu.VMEM((1, chunk), F32),
            pltpu.VMEM((1, vox), F32),
            pltpu.VMEM((tiles, slices + ONES, chunk), BF16),
            pltpu.VMEM((PASSES, tiles, slices + ONES, chunk), BF16),
            pltpu.VMEM((PASSES, slices + ONES, rays), BF16),
            pltpu.VMEM((hops, slices, SIDE), BF16),
            pltpu.VMEM((hops, slices, SIDE), BF16),
            pltpu.VMEM((hops, slices, vox), BF16),
            pltpu.VMEM((hops, slices, vox), BF16),
            pltpu.VMEM((slices, rays), F32),
            pltpu.VMEM((subsets, slices, vox), BF16),
            dma((rays // (GROUP * chunk),)),
            dma((4,)),
            dma((tiles,)),
            dma((PASSES, tiles)),
            dma((tiles,)),
            dma((PASSES, tiles)),
            dma((hops,)),
            dma((hops,)),
            dma((hops, chunks)),
            dma((hops, chunks)),
            dma((9, chunks)),
            dma((9, chunks)),
        ],
        compiler_params=pltpu.CompilerParams(
            collective_id=0, has_side_effects=True, vmem_limit_bytes=VMEM_LIMIT
        ),
    )(*(pltpu.with_memory_space_constraint(x, pltpu.HBM) for x in (order, pattern, start, meas, system)))


def body(tiles, chunks, start_volume, measured, system_values, block_pattern, subset_order):
    return sweep(
        tiles, chunks, jnp.transpose(subset_order), block_pattern, start_volume, measured, system_values
    )


def solution(mesh):
    placed = (
        P(None, None, "tile"),
        P("subset", None, None, None),
        P("subset", None, "tile"),
        P("subset", None, "tile"),
        P(),
    )
    return jax.shard_map(
        functools.partial(body, mesh.shape["tile"], 16),
        mesh=mesh, in_specs=placed, out_specs=P(None, None, "tile"), check_vma=False,
    )
```

```python
import functools

import jax
import jax.numpy as jnp
from jax import lax
from jax.experimental import pallas as pl
from jax.experimental.pallas import tpu as pltpu
from jax.sharding import PartitionSpec as P

MESH = pl.DeviceIdType.MESH
F32 = jnp.float32
BF16 = jnp.bfloat16
SIDE = 128
PASSES = 4
ONES = 16
NT = (((1,), (1,)), ((), ()))
NN = (((1,), (0,)), ((), ()))


TN = (((0,), (0,)), ((), ()))
LATE = 2
GROUP = 4
PIECE = 512
VMEM_LIMIT = 44 * 1024 * 1024


def bit(x, k):
    return lax.rem(lax.div(x, 2**k), 2)


def flip(x, d):
    for k in range(d.bit_length()):
        if d >> k & 1:
            x = x + 2**k * (1 - 2 * bit(x, k))
    return x


def differ(x, y, bits):
    return sum(2**k * lax.rem(bit(x, k) + bit(y, k), 2) for k in range(bits))


def dot(a, b, dims):
    return lax.dot_general(a, b, dims, preferred_element_type=F32)


def sweep_kernel(
    tiles, order_hbm, pattern_hbm, start_hbm, meas_hbm, sys_hbm, out_ref,
    turned_ref, order_ref, pick_ref, pattern_ref, mask_ref, a_ref, start_ref, vb_ref, meas_ref, dest_ref, rows_ref, inv_ref,
    part, recv, resid, mid_out, mid_in, hop_out, hop_in, acc, gat,
    a_sem, io_sem, rs_send, rs_recv, ag_send, ag_recv, mid_send, mid_recv, hop_send, hop_recv,
    fin_send, fin_recv,
):
    me_s, me_t = lax.axis_index("subset"), lax.axis_index("tile")
    subsets = order_ref.shape[1]
    slices = order_ref.shape[0]
    bits = (tiles - 1).bit_length()
    partners = sorted(range(1, tiles), key=lambda d: -(4 * (d >> 3) + 2 * (d >> 2 & 1) * (1 - (d >> 1 & 1)) + (d >> 1 & 1)))
    rays, vox = a_ref.shape
    chunk = rays // tiles
    pair = GROUP * chunk
    pairs = rays // pair
    chunks = hop_send.shape[1]
    width = vox // chunks

    chips = [d for d in partners if d % 2 == 0]
    others = [d + 1 for d in chips] + [1]

    def tile_at(d):
        return flip(me_t, d)

    def subset_at(d):
        return lax.rem(me_s + d, subsets)

    def remote(src, dst, send, recv_, s, t):
        return pltpu.make_async_remote_copy(
            src_ref=src, dst_ref=dst, send_sem=send, recv_sem=recv_,
            device_id=(s, t), device_id_type=MESH,
        )

    def cols(n):
        return pl.ds(pl.multiple_of(n * width, width), width)

    def rays_of(c):
        return pl.ds(pl.multiple_of(c * chunk, chunk), chunk)

    order_copy = pltpu.make_async_copy(order_hbm, turned_ref, io_sem.at[2])
    order_copy.start()
    pattern_copy = pltpu.make_async_copy(pattern_hbm.at[0], pattern_ref, io_sem.at[3])
    pattern_copy.start()
    start_copy = pltpu.make_async_copy(start_hbm, start_ref, io_sem.at[0])
    start_copy.start()
    half = lax.div(me_t, GROUP)

    def pair_at(i):
        return flip(differ(half, i, bits), max(pairs - 2, 0))

    def block_rows(i):
        return pl.ds(pl.multiple_of(pair_at(i) * pair, pair), pair)

    def matrix_copy(i):
        return pltpu.make_async_copy(
            sys_hbm.at[0, block_rows(i), :], a_ref.at[block_rows(i), :], a_sem.at[i]
        )

    for i in range(pairs):
        matrix_copy(i).start()
    meas_copy = pltpu.make_async_copy(
        meas_hbm.at[0, :, :, rays_of(me_t)], meas_ref, io_sem.at[1]
    )
    meas_copy.start()

    barrier = pltpu.get_barrier_semaphore()
    for d in range(1, tiles):
        pl.semaphore_signal(barrier, inc=1, device_id=(me_s, tile_at(d)), device_id_type=MESH)
    for d in range(1, subsets):
        pl.semaphore_signal(barrier, inc=1, device_id=(subset_at(d), me_t), device_id_type=MESH)

    vb_ref[slices:, :] = jnp.ones((ONES, vox), BF16)
    resid[0, slices:, :] = jnp.ones((ONES, rays), BF16)

    def wide(x):
        return jnp.concatenate([x] * (width // x.shape[1]), axis=1)

    def hits(source):
        return [
            jnp.broadcast_to((order_ref[:, f : f + 1] == source).astype(F32), (slices, SIDE)).astype(BF16)
            for f in range(subsets)
        ]

    def select_start(source):
        weights = hits(source)

        @pl.loop(0, chunks)
        def _(n):
            total = wide(weights[0]) * start_ref[0, :, cols(n)]
            for f in range(1, subsets):
                total += wide(weights[f]) * start_ref[f, :, cols(n)]
            vb_ref[:slices, cols(n)] = total

    pattern_copy.wait()
    blocks = pattern_ref.shape[1]
    spread = lax.broadcasted_iota(jnp.int32, (blocks, vox), 1) // SIDE == lax.broadcasted_iota(
        jnp.int32, (blocks, vox), 0
    )
    mask_ref[...] = dot(
        pattern_ref[...].astype(F32).astype(BF16), spread.astype(F32).astype(BF16), NN
    )
    order_copy.wait()
    same = lax.broadcasted_iota(jnp.int32, (subsets, subsets), 0) == lax.broadcasted_iota(
        jnp.int32, (subsets, subsets), 1
    )
    order_ref[...] = dot(
        turned_ref[...].astype(F32).astype(BF16), same.astype(F32).astype(BF16), TN
    ).astype(jnp.int32)
    start_copy.wait()
    select_start(me_s)

    pl.semaphore_wait(barrier, tiles - 1 + subsets - 1)

    def rs_copy(j, d, c, height, block=None):
        block = c if block is None else block
        return remote(
            part.at[block, pl.ds(0, height), :], recv.at[j, d, pl.ds(0, height), :],
            rs_send.at[d], rs_recv.at[j, d], me_s, c,
        )

    @pl.loop(0, pairs)
    def _(i):
        matrix_copy(i).wait()
        b = pair_at(i)
        per_pair = pair // SIDE
        piece = min(PIECE, vox)
        p = jnp.zeros((slices + ONES, pair), F32)
        for k in range(0, vox, piece):
            parts = []
            for q in range(per_pair):
                mask = jnp.broadcast_to(mask_ref[pl.ds(b * per_pair + q, 1), k : k + piece], (16, piece)).astype(BF16)
                here = pl.ds(pl.multiple_of(b * pair + q * SIDE, SIDE), SIDE)
                masked = a_ref[here, k : k + piece] * jnp.concatenate([mask] * (SIDE // 16), axis=0)
                a_ref[here, k : k + piece] = masked
                parts.append(masked)
            p += dot(vb_ref[:, k : k + piece], jnp.concatenate(parts, axis=0), NT)
        sums = p[slices:, :]
        high = sums.astype(BF16)
        rest = sums - high.astype(F32)
        mid = rest.astype(BF16)
        low = (rest - mid.astype(F32)).astype(BF16)
        row = lax.broadcasted_iota(jnp.int32, sums.shape, 0)
        packed = jnp.where(
            row == 0, high.astype(F32),
            jnp.where(row == 1, mid.astype(F32), jnp.where(row == 2, low.astype(F32), 0.0)),
        ).astype(BF16)
        for h in range(GROUP):
            c = GROUP * b + h
            part[c, pl.ds(0, slices), :] = p[:slices, h * chunk : (h + 1) * chunk].astype(BF16)
            part[c, pl.ds(slices, ONES), :] = packed[:, h * chunk : (h + 1) * chunk]
            d = differ(c, me_t, bits)

            @pl.when(d != 0)
            def _():
                rs_copy(0, d, c, slices + ONES).start()

    half_slices = slices // 2
    side = subsets * half_slices
    column = lax.broadcasted_iota(jnp.int32, (half_slices, side), 1)
    row = lax.broadcasted_iota(jnp.int32, (half_slices, side), 0)
    for h in range(2):
        for f in range(subsets):
            last = lax.rem(order_ref[h * half_slices : (h + 1) * half_slices, f : f + 1] + (PASSES - 1), subsets)
            hit = column == last * half_slices + row
            pick_ref[h, f * half_slices : (f + 1) * half_slices, :] = hit.astype(F32).astype(BF16)

    meas_copy.wait()
    for j in range(PASSES):
        source = lax.rem(me_s + subsets - j, subsets)
        total = jnp.zeros((slices, chunk), F32)
        for f in range(subsets):
            weight = (order_ref[:, f : f + 1] == source).astype(F32)
            total += weight * meas_ref[f].astype(F32)
        dest_ref[j] = total

    def ag_copy(j, d):
        here = resid.at[j, pl.ds(0, slices), rays_of(me_t)]
        return remote(here, here, ag_send.at[d], ag_recv.at[j, d], me_s, tile_at(d))

    def ag_arrival(j, d):
        here = resid.at[j, pl.ds(0, slices), rays_of(tile_at(d))]
        return remote(here, here, ag_send.at[d], ag_recv.at[j, d], me_s, tile_at(d))

    def hop_copy(j, n):
        return remote(
            hop_out.at[j, :, cols(n)], hop_in.at[j, :, cols(n)],
            hop_send.at[j, n], hop_recv.at[j, n], subset_at(1), me_t,
        )

    def mid_copy(j):
        return remote(
            mid_out.at[j], mid_in.at[j], mid_send.at[j], mid_recv.at[j], subset_at(1), me_t
        )

    def change_so_far(j, n):
        return hop_in[j - 1, :, cols(n)].astype(F32) + wide(mid_in[j - 1].astype(F32))

    zp = me_s + 1 - 2 * lax.rem(me_s, 2)
    yp, ym, y2 = subset_at(2), subset_at(subsets - 2), subset_at(subsets // 2)
    zp_p = lax.rem(zp + 2, subsets)
    zp_m = lax.rem(zp + subsets - 2, subsets)
    zp_2 = lax.rem(zp + subsets // 2, subsets)

    def fin_copy(kind, block, n, target):
        here = gat.at[block, :, cols(n)]
        return remote(here, here, fin_send.at[kind, n], fin_recv.at[kind, n], target, me_t)

    for j in range(PASSES):
        height = slices + ONES if j == 0 else slices
        if j > 0:
            acc[...] = jnp.zeros_like(acc)
            mid_copy(j - 1).wait_recv()

            @pl.loop(0, chunks)
            def _(n):
                hop_copy(j - 1, n).wait_recv()
                volume = vb_ref[:slices, cols(n)].astype(F32) + change_so_far(j, n)
                acc[...] += dot(volume.astype(BF16), a_ref[:, cols(n)], NT)

            for d in others:
                part[tile_at(d), pl.ds(0, slices), :] = acc[:, rays_of(tile_at(d))].astype(BF16)
                rs_copy(j, d, tile_at(1), slices, tile_at(d)).start()
            for d in chips:
                rs_copy(j, d + 1, tile_at(1), slices).wait_recv()
                both = acc[:, rays_of(tile_at(d))] + recv[j, d + 1, pl.ds(0, slices), :].astype(F32)
                part[tile_at(d), pl.ds(0, slices), :] = both.astype(BF16)
                rs_copy(j, d, tile_at(d), slices).start()

        if j + 1 < PASSES:
            select_start(lax.rem(me_s + subsets - j - 1, subsets))

        if j == 0:
            total = part[me_t].astype(F32)
        else:
            rs_copy(j, 1, tile_at(1), slices).wait_recv()
            total = acc[:, rays_of(me_t)] + recv[j, 1, pl.ds(0, slices), :].astype(F32)
        for d in reversed(partners if j == 0 else chips):
            rs_copy(j, d, tile_at(d), height).wait_recv()
            total += recv[j, d, pl.ds(0, height), :].astype(F32)
        if j == 0:
            rows_ref[...] = jnp.sum(total[slices:, :], axis=0, keepdims=True)
        value = (dest_ref[j] - total[:slices, :]) / rows_ref[...]
        resid[j, pl.ds(0, slices), rays_of(me_t)] = value.astype(BF16)
        for d in partners:
            ag_copy(j, d).start()
        for d in range(1, tiles):
            rs_copy(j, d, tile_at(d), height).wait_send()
        for d in range(1, tiles):
            ag_arrival(j, d).wait_recv()

        @pl.loop(0, chunks)
        def _(n):
            here = cols(n)
            if j == 0:
                back = dot(resid[0], a_ref[:, here], NN)
                inv = 1.0 / back[slices : slices + 1, :]
                inv_ref[:, here] = inv
                change = back[:slices, :] * inv
            else:
                back = dot(resid[j, pl.ds(0, slices), :], a_ref[:, here], NN)
                change = change_so_far(j, n) + back * inv_ref[:, here]
            if j + 1 < PASSES:
                @pl.when(n == 0)
                def _():
                    mean = jnp.sum(change, axis=1, keepdims=True) * (1.0 / width)
                    mid_out[j] = jnp.broadcast_to(mean, mid_out.shape[1:]).astype(BF16)
                    mid_copy(j).start()

                hop_out[j, :, here] = (change - wide(mid_out[j].astype(F32))).astype(BF16)
                hop_copy(j, n).start()
            else:
                gat[me_s, :, here] = (vb_ref[:slices, here].astype(F32) + change).astype(BF16)
                fin_copy(0, me_s, n, zp).start()
                fin_copy(1, me_s, n, yp).start()
                fin_copy(2, me_s, n, ym).start()

        for d in range(1, tiles):
            ag_copy(j, d).wait_send()

    late = min(LATE, chunks - 1)

    @pl.loop(0, chunks)
    def _(n):
        fin_copy(1, ym, n, me_s).wait_recv()
        fin_copy(2, yp, n, me_s).wait_recv()

        @pl.when(lax.rem(n, 2) == 0)
        def _():
            fin_copy(3, ym, n, yp).start()

        @pl.when(lax.rem(n, 2) == 1)
        def _():
            fin_copy(3, yp, n, ym).start()

        @pl.when(n < late)
        def _():
            fin_copy(7, ym, n, zp).start()
            fin_copy(8, yp, n, zp).start()

    @pl.loop(0, chunks)
    def _(n):
        fin_copy(0, zp, n, me_s).wait_recv()

        @pl.when(n >= late)
        def _():
            fin_copy(4, zp, n, yp).start()
            fin_copy(5, zp, n, ym).start()

    @pl.loop(0, chunks)
    def _(n):
        fin_copy(3, y2, n, me_s).wait_recv()
        fin_copy(6, y2, n, zp).start()

    @pl.loop(0, chunks)
    def _(n):
        @pl.when(n < late)
        def _():
            fin_copy(7, zp_m, n, me_s).wait_recv()
            fin_copy(8, zp_p, n, me_s).wait_recv()

        @pl.when(n >= late)
        def _():
            fin_copy(4, zp_m, n, me_s).wait_recv()
            fin_copy(5, zp_p, n, me_s).wait_recv()

        fin_copy(6, zp_2, n, me_s).wait_recv()
        for h in range(2):
            there = pl.ds(h * half_slices, half_slices)
            rows = gat[:, there, cols(n)].reshape(side, width)
            placed = dot(pick_ref[h], rows, NN).astype(BF16)
            out_ref[:, there, cols(n)] = placed.reshape(subsets, half_slices, width)

    @pl.loop(0, chunks)
    def _(n):
        for kind in (0, 1, 2, 3, 6):
            fin_copy(kind, me_s, n, zp).wait_send()

        @pl.when(n < late)
        def _():
            fin_copy(7, me_s, n, zp).wait_send()
            fin_copy(8, me_s, n, zp).wait_send()

        @pl.when(n >= late)
        def _():
            fin_copy(4, me_s, n, zp).wait_send()
            fin_copy(5, me_s, n, zp).wait_send()

        for j in range(PASSES - 1):
            hop_copy(j, n).wait_send()

    for j in range(PASSES - 1):
        mid_copy(j).wait_send()


def sweep(tiles, chunks, order, pattern, start, meas, system):
    subsets, slices, vox = start.shape
    rays = system.shape[1]
    chunk = rays // tiles
    hops = PASSES - 1
    dma = pltpu.SemaphoreType.DMA
    hbm = pl.BlockSpec(memory_space=pltpu.HBM)
    return pl.pallas_call(
        functools.partial(sweep_kernel, tiles),
        out_shape=jax.ShapeDtypeStruct((subsets, slices, vox), BF16),
        in_specs=[hbm] * 5,
        out_specs=pl.BlockSpec(memory_space=pltpu.VMEM),
        scratch_shapes=[
            pltpu.VMEM(order.shape, jnp.int32),
            pltpu.VMEM(order.shape[::-1], jnp.int32),
            pltpu.VMEM((2, subsets * slices // 2, subsets * slices // 2), BF16),
            pltpu.VMEM(pattern.shape[1:], jnp.int32),
            pltpu.VMEM((pattern.shape[1], vox), F32),
            pltpu.VMEM((rays, vox), BF16),
            pltpu.VMEM((subsets, slices, vox), BF16),
            pltpu.VMEM((slices + ONES, vox), BF16),
            pltpu.VMEM((subsets, slices, chunk), BF16),
            pltpu.VMEM((PASSES, slices, chunk), F32),
            pltpu.VMEM((1, chunk), F32),
            pltpu.VMEM((1, vox), F32),
            pltpu.VMEM((tiles, slices + ONES, chunk), BF16),
            pltpu.VMEM((PASSES, tiles, slices + ONES, chunk), BF16),
            pltpu.VMEM((PASSES, slices + ONES, rays), BF16),
            pltpu.VMEM((hops, slices, SIDE), BF16),
            pltpu.VMEM((hops, slices, SIDE), BF16),
            pltpu.VMEM((hops, slices, vox), BF16),
            pltpu.VMEM((hops, slices, vox), BF16),
            pltpu.VMEM((slices, rays), F32),
            pltpu.VMEM((subsets, slices, vox), BF16),
            dma((rays // (GROUP * chunk),)),
            dma((4,)),
            dma((tiles,)),
            dma((PASSES, tiles)),
            dma((tiles,)),
            dma((PASSES, tiles)),
            dma((hops,)),
            dma((hops,)),
            dma((hops, chunks)),
            dma((hops, chunks)),
            dma((9, chunks)),
            dma((9, chunks)),
        ],
        compiler_params=pltpu.CompilerParams(
            collective_id=0, has_side_effects=True, vmem_limit_bytes=VMEM_LIMIT
        ),
    )(*(pltpu.with_memory_space_constraint(x, pltpu.HBM) for x in (order, pattern, start, meas, system)))


def body(tiles, chunks, start_volume, measured, system_values, block_pattern, subset_order):
    return sweep(
        tiles, chunks, jnp.transpose(subset_order), block_pattern, start_volume, measured, system_values
    )


def solution(mesh):
    placed = (
        P(None, None, "tile"),
        P("subset", None, None, None),
        P("subset", None, "tile"),
        P("subset", None, "tile"),
        P(),
    )
    return jax.shard_map(
        functools.partial(body, mesh.shape["tile"], 16),
        mesh=mesh, in_specs=placed, out_specs=P(None, None, "tile"), check_vma=False,
    )
```
